256 devices in a mesh: psg: 128 (over y, z, x), qry: 2 (over core).
Axes of the slice: x: 4, y: 4, z: 8, core: 2. Of those that a mesh axis runs over, the one named last changes fastest.
Arguments:
- queries: bfloat16 [2048, 32, 128], P(('psg', 'qry')), may hold values from -0.59765625 to 0.59765625
- cand_shard: int32 [2048, 256, 1], P(('psg', 'qry')), may hold values from 0 to 255; in each aligned block of 256 rows (0 to 255, 256 to 511, ..., all dimensions but the last counted through in order) at most 2 rows name the same one
- cand_local: int32 [2048, 256], P(('psg', 'qry')), may hold values from 0 to 63
- passages: bfloat16 [16384, 70, 128], P(('psg', 'qry')), may hold values from -0.59765625 to 0.59765625
- lengths: int32 [16384], P(('psg', 'qry')), may hold values from 8 to 70
Outputs:
- scores: float32 [2048, 256], P(('psg', 'qry'))
The draws below stay inside these ranges and needn't reach their ends.
Inputs may be any that keep to these rules, and one draw needn't show every extreme that they name: `cand_shard`: among the 256 candidates of one query no device is named more than 2 times, and some query names some device exactly 2 times; some devices hold far more candidates than others.
All inputs are finite; a program needn't handle non-finite values.
Results may differ from the reference program's by a relative error of at most 0.0003.
Values may be sent and summed in bfloat16 or wider, within the bound.
A program may use at most 128 MiB of HBM per device.

```python
import math
import jax
import jax.numpy as jnp
import numpy as np
from jax import lax

DIM = 128
QLEN = 32
PLEN = 70
POOL = 256
P_DEV = 64
QCAP = 2
QUERIES = 2048
PASSAGES = 16384
N_PSG = 128
N_QRY = 2


def touch_ends(values, rng, smallest, top_value):
    place = [jax.random.randint(jax.random.fold_in(rng, axis), (), 0, length) for axis, length in enumerate(values.shape)]
    main_axis = values.shape.index(max(values.shape))
    neighbour = place[:main_axis] + [(place[main_axis] + 1) % values.shape[main_axis]] + place[main_axis + 1:]
    return values.at[tuple(place)].set(smallest).at[tuple(neighbour)].set(top_value)


def level_of(rng, dims, shards, low, high):
    loudness = 1.0
    for position, shards_of in shards:
        heights = jax.random.uniform(jax.random.fold_in(jax.random.fold_in(rng, 6), position), (shards_of,), jnp.float32, low / len(shards), high / len(shards))
        loudness = loudness * jnp.repeat(jnp.exp(heights), dims[position] // shards_of).reshape((-1,) + (1,) * (len(dims) - 1 - position))
    return loudness


def assign_block(own_key, own, number, rows, number_of, top, limit, lean):
    order = jax.random.permutation(own_key, number_of)
    crowded, usual = shares(number_of, rows * top, limit, lean, True), shares(number_of, rows * top, limit, lean, False)
    places = jnp.arange(number_of)

    def named(sizes, rotation):
        used = int((sizes > 0).sum())
        fixed = max(1, used // 4)
        shifted = fixed + (places - fixed + rotation * (used - fixed)) % max(1, number_of - fixed)
        return jnp.zeros((number_of,), jnp.int32).at[order[jnp.where(places < fixed, places, shifted)]].set(jnp.asarray(sizes, jnp.int32))

    sizes = jnp.where(number % 4 == 0, named(crowded, number // 4), named(usual, number - number // 4 - 1))
    mixed = jax.random.permutation(jax.random.fold_in(own, 3), number_of)
    giver, receiver = mixed[0:number_of // 2 * 2:2], mixed[1:number_of // 2 * 2:2]
    margin = jnp.minimum(sizes[giver] - 1, limit - sizes[receiver]) // 2
    margin = jnp.where((giver == order[0]) | (receiver == order[0]) | (sizes[receiver] == 0), 0, jnp.maximum(margin, 0))
    shifted = jax.random.randint(jax.random.fold_in(own, 4), (number_of // 2,), 0, 1 << 20) % (margin + 1)
    sizes = sizes.at[giver].add(-shifted).at[receiver].add(shifted)
    labels = jnp.searchsorted(jnp.cumsum(sizes), jnp.arange(rows * top), side="right").astype(jnp.int32)
    table = labels.reshape(top, rows).T
    table = table[jax.random.permutation(jax.random.fold_in(own, 1), rows)]
    rotation = jax.random.randint(jax.random.fold_in(own, 2), (rows, 1), 0, top)
    return jnp.take_along_axis(table, (jnp.arange(top)[None, :] + rotation) % top, axis=1)


def shares(amount, total, limit, skew, full):
    loads = [(1 << 20) // math.isqrt(standing ** skew) + 1 for standing in range(1, amount + 1)]
    largest = limit if full else min(limit, max(-(-total // amount), total * loads[0] // sum(loads)))
    least = 1 if total - largest >= amount - 1 else 0
    holding, spare = [largest] + [least] * (amount - 1), total - largest - least * (amount - 1)
    while spare > 0:
        free = [i for i in range(1, amount) if holding[i] < largest] or [i for i in range(1, amount) if holding[i] < limit]
        pool, budget = sum([loads[i] for i in free]), spare
        for i in free:
            more = min(limit - holding[i], max(1, budget * loads[i] // pool), spare)
            holding[i] = holding[i] + more
            spare = spare - more
    return np.array(holding)


def scatter_about(key, shape, width, reach, cuts=(), held_as=jnp.bfloat16):
    array = jax.random.normal(key, shape, jnp.float32) * width
    if len(cuts) > 0:
        array = level_of(key, shape, cuts, -0.22, 0.18) * array
    return jnp.clip(array, min=-reach, max=reach).astype(held_as)


def setup_inputs(seed: int = 0) -> dict:
    arg_keys = jax.random.split(jax.random.key(seed), 6)
    queries = scatter_about(arg_keys[0], (QUERIES, QLEN, DIM), 0.1, 0.59765625, ((0, 256),))
    cand_shard_keys = jax.random.split(jax.random.fold_in(arg_keys[1], 1), QUERIES * POOL // POOL)
    cand_shard_turns = jax.random.permutation(jax.random.fold_in(arg_keys[1], 3), QUERIES * POOL // POOL)
    cand_shard = jax.vmap(lambda own, number: assign_block(jax.random.fold_in(arg_keys[1], 2), own, number, POOL, N_PSG * N_QRY, 1, QCAP, 2))(cand_shard_keys, cand_shard_turns).reshape((QUERIES, POOL, 1))
    cand_local = touch_ends(jax.random.randint(arg_keys[2], (QUERIES, POOL), 0, P_DEV), jax.random.fold_in(arg_keys[2], 1), 0, P_DEV - 1).astype(jnp.int32)
    passages = scatter_about(arg_keys[3], (PASSAGES, PLEN, DIM), 0.1, 0.59765625, ((0, 256),))
    lengths = touch_ends(jax.random.randint(arg_keys[4], (PASSAGES,), PLEN // 8, PLEN + 1), jax.random.fold_in(arg_keys[4], 1), PLEN // 8, PLEN).astype(jnp.int32)
    return {"queries": queries, "cand_shard": cand_shard, "cand_local": cand_local, "passages": passages, "lengths": lengths}


def pair_scores(query_tile_block, passage_tile_block, token_counts):
    token_similarity = jnp.einsum("ajs,aeks->aejk", query_tile_block.astype(jnp.float32), passage_tile_block.astype(jnp.float32))
    positions = jnp.arange(passage_tile_block.shape[2], dtype=jnp.int32)
    valid_tokens = positions[None, None, None, :] < token_counts[:, :, None, None]
    return jnp.sum(jnp.max(jnp.where(valid_tokens, token_similarity, -1e30), axis=3), axis=2)


def reference(queries, cand_shard, cand_local, passages, lengths):
    passage_row = (cand_shard[:, :, 0] * P_DEV + cand_local).astype(jnp.int32)
    block_rows = 8
    block_count = QUERIES // block_rows

    def single_block(tiles):
        query_tile_block, rows_block = tiles
        return pair_scores(query_tile_block, passages[rows_block], lengths[rows_block])

    rescored_output = lax.map(single_block, (queries.reshape(block_count, block_rows, QLEN, DIM), passage_row.reshape(block_count, block_rows, POOL)))
    return rescored_output.reshape(QUERIES, POOL)
```

```python
import functools
import heapq

import jax
import jax.numpy as jnp
from jax import lax
from jax.experimental import pallas as pl
from jax.experimental.pallas import tpu as pltpu
from jax.sharding import PartitionSpec as P

MESH = pl.DeviceIdType.MESH
RING = {"y": 4, "z": 8, "x": 4}
CHIPS = 128
ROWS = 80
SLOTS = 4
STREAMS = ((0, 2, "xyz"), (2, 3, "yzx"), (5, 3, "xzy"))


def offsets(n):
    out = [0]
    for k in range(1, n // 2):
        out += [k, -k]
    return out + [n // 2]


def plan():
    copies = {}
    for c, (_, nq, order) in enumerate(STREAMS):
        n1, n2, n3 = (RING[a] for a in order)
        first = [(c, 1, d, h, 0) for d in (1, -1) for h in range(1, n1 // 2 + 1)]
        for d in (1, -1):
            for h in range(1, n1 // 2 + 1):
                copies[c, 1, d, h, 0] = ([(c, 1, d, h - 1, 0)] if h > 1 else [], nq / (2 if h == n1 // 2 else 1), order[0])
            for h in range(1, n2 // 2 + 1):
                copies[c, 2, d, h, 0] = ([(c, 2, d, h - 1, 0)] if h > 1 else first, nq * n1 / (2 if h == n2 // 2 else 1), order[1])
            for h in range(1, n3 // 2 + 1):
                for j, off in enumerate(offsets(n2)):
                    if h == n3 // 2 and (j % 2 == 0) != (d == 1):
                        continue
                    if h > 1:
                        needs = [(c, 3, d, h - 1, j)]
                    elif off == 0:
                        needs = first
                    elif off == n2 // 2:
                        needs = [(c, 2, e, off, 0) for e in (1, -1)]
                    else:
                        needs = [(c, 2, -1 if off > 0 else 1, abs(off), 0)]
                    copies[c, 3, d, h, j] = (needs, nq * n1, order[2])
    waiting = {key: set(needs) for key, (needs, _, _) in copies.items()}
    free, arrivals, order = {}, [], []

    def issue(key, now):
        _, size, axis = copies[key]
        link = axis, key[2]
        free[link] = max(free.get(link, 0.0), now) + size * 0.177
        heapq.heappush(arrivals, (free[link] + 1.7, len(order), key))

    for key in copies:
        if not waiting[key]:
            issue(key, 0.0)
    while arrivals:
        now, _, key = heapq.heappop(arrivals)
        order.append((key, now))
        for other, needs in waiting.items():
            if key in needs:
                needs.discard(key)
                if not needs:
                    issue(other, now)
    return copies, order


def spread_kernel(compute, q_ref, tab_ref, pp_ref, out_ref, ga, gb, gc, pp, tabv, tabs, best, total, got,
                  send, recv, aux, far):
    me, core = lax.axis_index("psg"), lax.axis_index("qry")
    m = {"x": lax.rem(me, 4), "z": lax.rem(me // 4, 8), "y": me // 32}
    gathered = (ga, gb, gc)
    copies, order = plan()
    number = {key: i for i, key in enumerate(copies)}

    def chip(axis, d):
        at = dict(m)
        at[axis] = lax.rem(m[axis] + (d + RING[axis]), RING[axis])
        return (at["y"] * 8 + at["z"]) * 4 + at["x"]

    def piece(key, sent):
        c, phase, d, h, j = key
        _, nq, axes = STREAMS[c]
        n1, n2, n3 = (RING[a] for a in axes)
        g, n, axis = gathered[c], (n1, n2, n3)[phase - 1], axes[phase - 1]
        unit = lax.rem(m[axis] + (n - d * (h - 1 if sent else h)), n)
        half = h == n // 2
        m1, m2, m3 = (m[a] for a in axes)
        if phase == 1:
            some = (pl.ds(0, nq // 2) if d == 1 else pl.ds(nq // 2, nq - nq // 2)) if half else pl.ds(0, nq)
            return g.at[m3, m2, unit, some]
        if phase == 2:
            some = pl.ds(0 if d == 1 else n1 // 2, n1 // 2) if half else pl.ds(0, n1)
            return g.at[m3, unit, some]
        return g.at[unit, lax.rem(m2 + (offsets(n2)[j] + n2), n2)]

    def remote(key, sent):
        c, phase, d, h, _ = key
        ref = piece(key, sent)
        source = ref
        if phase == 1 and h == 1 and sent:
            q0, nq, _ = STREAMS[c]
            source = q_ref.at[pl.ds(q0, nq)]
        return pltpu.make_async_remote_copy(
            src_ref=source, dst_ref=ref, send_sem=send.at[number[key]], recv_sem=recv.at[number[key]],
            device_id=(chip(STREAMS[c][2][phase - 1], d), core), device_id_type=MESH)

    waiting = {key: set(needs) for key, (needs, _, _) in copies.items()}
    for key in copies:
        if not waiting[key]:
            remote(key, True).start()

    stay = []
    for c, (q0, nq, axes) in enumerate(STREAMS):
        m1, m2, m3 = (m[a] for a in axes)
        stay.append(pltpu.make_async_copy(q_ref.at[pl.ds(q0, nq)], gathered[c].at[m3, m2, m1], aux.at[c]))
    stay.append(pltpu.make_async_copy(pp_ref, pp.at[pl.ds(core * 64, 64)], aux.at[3]))
    stay.append(pltpu.make_async_copy(tab_ref.at[pl.ds(me, 1)], tabv.at[pl.ds(me, 1)], aux.at[4]))
    for copy in stay:
        copy.start()

    def to_all(source, target, s, r):
        def one(k, _):
            other = lax.rem(me + k, CHIPS)
            pltpu.make_async_remote_copy(
                src_ref=source(other), dst_ref=target.at[pl.ds(me, 1)], send_sem=s, recv_sem=r,
                device_id=(other, core), device_id_type=MESH).start()
            return 0
        lax.fori_loop(1, CHIPS, one, 0)

    def all_done(ref, sem):
        rows = ref.at[pl.ds(0, CHIPS - 1)]
        pltpu.make_async_copy(rows, rows, sem).wait()

    to_all(lambda other: tab_ref.at[pl.ds(other, 1)], tabv, far.at[0], far.at[1])
    partner = pltpu.make_async_remote_copy(
        src_ref=pp_ref, dst_ref=pp.at[pl.ds(core * 64, 64)], send_sem=far.at[2], recv_sem=far.at[3],
        device_id=(me, 1 - core), device_id_type=MESH)
    partner.start()
    for copy in stay:
        copy.wait()

    lane = lax.broadcasted_iota(jnp.int32, (8, 128), 1)
    zero = jnp.zeros((32, 128), jnp.bfloat16)

    def score(c, y, z, u):
        line = y * 8 + z
        _, _, axes = STREAMS[c]
        q = STREAMS[c][0] + u
        at = {"y": y, "z": z}
        tiles = []
        for x in range(4):
            at["x"] = x
            tiles.append(gathered[c][at[axes[2]], at[axes[1]], at[axes[0]], u])
        w = jnp.concatenate(
            [jnp.concatenate([t, zero] if x % 2 == 0 else [zero, t], 1) for x, t in enumerate(tiles)], 0)
        sides = []
        for x in (0, 1):
            sides.append(jnp.concatenate(
                [pp[tabs[line * 4 + x + 2 * h, q * SLOTS + s]] for s in range(SLOTS) for h in range(2)], 0))
        o = lax.dot_general(jnp.concatenate(sides, 1), w, (((1,), (1,)), ((), ())), preferred_element_type=jnp.float32)
        for s in range(SLOTS):
            pair = [jnp.max(o[(2 * s + h) * ROWS:(2 * s + h + 1) * ROWS].reshape(ROWS // 8, 8, 128), axis=0) for h in range(2)]
            top = jnp.max(jnp.where(lane < 64, pair[0], pair[1]), axis=0, keepdims=True)
            best[q * SLOTS + s, pl.ds(line, 1), :] = top

    def around(axis, k):
        return lax.rem(m[axis] + (k + RING[axis]), RING[axis])

    def part(i, n):
        return lax.rem(i, n), i // n

    def blocks():
        out = []
        all1 = [key for key in copies if key[0] == 0 and key[1] < 3]

        def own0(i):
            u, y = part(i, 2)
            score(0, y, m["z"], u)
        out.append((all1, 8, own0))
        for h in range(1, 5):
            needs = [key for key in copies if key[0] == 0 and key[1] == 3 and key[3] == h]

            def far0(i, h=h):
                u, i = part(i, 2)
                y, sign = part(i, 4)
                score(0, y, lax.rem(m["z"] + 8 + h - 2 * h * sign, 8), u)
            out.append((needs, 16 if h < 4 else 8, far0))
        all2 = [key for key in copies if key[0] == 2 and key[1] < 3]

        def own2(i):
            u, z = part(i, 3)
            score(2, m["y"], z, u)
        out.append((all2, 24, own2))
        offs = offsets(8)
        for j in range(0, 8, 2):
            def hop2(i, j=j):
                u, i = part(i, 3)
                which, sign = part(i, 2)
                z = lax.rem(m["z"] + 8 + jnp.where(which == 0, offs[j], offs[j + 1]), 8)
                score(2, lax.rem(m["y"] + 4 + 1 - 2 * sign, 4), z, u)
            out.append(([key for key in copies if key[0] == 2 and key[1:2] == (3,) and key[3] == 1 and key[4] in (j, j + 1)], 12, hop2))
        for j in range(0, 8, 4):
            def last2(i, j=j):
                u, w = part(i, 3)
                off = jnp.where(w < 2, jnp.where(w == 0, offs[j], offs[j + 1]), jnp.where(w == 2, offs[j + 2], offs[j + 3]))
                score(2, around("y", 2), lax.rem(m["z"] + 8 + off, 8), u)
            out.append(([key for key in copies if key[0] == 2 and key[1] == 3 and key[3] == 2 and j <= key[4] < j + 4], 12, last2))
        for j in range(8):
            def line1(i, j=j):
                u, y = part(i, 3)
                score(1, y, lax.rem(m["z"] + 8 + offs[j], 8), u)
            needs = [key for key in copies if key[0] == 1 and key[1] == 3 and key[4] == j]
            needs += [key for key in copies if key[0] == 1 and key[1] < 3]
            out.append((needs, 12, line1))
        return out

    todo = [(set(needs), n, f) for needs, n, f in blocks()]
    ready, started, clock = [], False, 0.0

    def run(job):
        _, n, f = job
        unroll = 4

        def some(i, _):
            for k in range(unroll):
                f(i * unroll + k)
            return 0
        lax.fori_loop(0, n // unroll, some, 0)

    for key, now in order:
        while compute and ready and clock < now:
            if not started:
                all_done(tabv, far.at[1])
                partner.wait_recv()
                copy = pltpu.make_async_copy(tabv, tabs, aux.at[5])
                copy.start()
                copy.wait()
                started = True
            job = ready.pop(0)
            run(job)
            clock = max(clock, 0.0) + 0.13 * job[1]
        clock = max(clock, now)
        remote(key, False).wait_recv()
        for other, needs in waiting.items():
            if key in needs:
                needs.discard(key)
                if not needs:
                    remote(other, True).start()
        for job in todo:
            if key in job[0]:
                job[0].discard(key)
                if not job[0]:
                    ready.append(job)
    if not started:
        all_done(tabv, far.at[1])
        partner.wait_recv()
        copy = pltpu.make_async_copy(tabv, tabs, aux.at[5])
        copy.start()
        copy.wait()
    if compute:
        for job in ready:
            run(job)
    lanes = lax.broadcasted_iota(jnp.int32, (32, 128), 1) % 32
    sums = jnp.zeros((32, 128), jnp.float32)
    for v in range(32):
        s = best[v]
        for step in (16, 8, 4, 2, 1):
            s = s + pltpu.roll(s, 128 - step, 1)
        sums = jnp.where(lanes == v, pltpu.roll(s, v, 1) if v else s, sums)
    total[...] = sums
    to_all(lambda other: total.at[pl.ds(other // 4, 1)], got, far.at[4], far.at[5])
    mine = pltpu.make_async_copy(total.at[pl.ds(me // 4, 1)], got.at[pl.ds(me, 1)], aux.at[6])
    mine.start()
    for key in copies:
        remote(key, True).wait_send()
    partner.wait_send()
    all_done(tabv, far.at[0])
    mine.wait()
    all_done(got, far.at[4])
    all_done(got, far.at[5])
    out_ref[...] = got[...]


def spread(q, tab, passages, compute=True):
    n = len(plan()[0])
    vmem = pl.BlockSpec(memory_space=pltpu.VMEM)
    scratch = []
    for _, nq, axes in STREAMS:
        scratch.append(pltpu.VMEM((RING[axes[2]], RING[axes[1]], RING[axes[0]], nq, 32, 128), jnp.bfloat16))
    scratch += [
        pltpu.VMEM((128, ROWS, 128), jnp.bfloat16),
        pltpu.VMEM((CHIPS, 128), jnp.int32),
        pltpu.SMEM((CHIPS, 128), jnp.int32),
        pltpu.VMEM((32, 32, 128), jnp.float32),
        pltpu.VMEM((32, 128), jnp.float32),
        pltpu.VMEM((CHIPS, 128), jnp.float32),
        pltpu.SemaphoreType.DMA((n,)),
        pltpu.SemaphoreType.DMA((n,)),
        pltpu.SemaphoreType.DMA((8,)),
        pltpu.SemaphoreType.DMA((8,)),
    ]
    return pl.pallas_call(
        functools.partial(spread_kernel, compute),
        out_shape=jax.ShapeDtypeStruct((CHIPS, 128), jnp.float32),
        in_specs=[vmem, vmem, vmem],
        out_specs=vmem,
        scratch_shapes=scratch,
        compiler_params=pltpu.CompilerParams(has_side_effects=True, vmem_limit_bytes=48 * 2**20),
        name="spread",
    )(q, tab, passages)


def matches(chip_row, upper):
    hit = lax.broadcasted_iota(jnp.int32, (CHIPS, 256), 0) == chip_row
    rank = jnp.dot(jnp.where(hit, 1.0, 0.0).astype(jnp.bfloat16), upper, preferred_element_type=jnp.float32)
    return hit, rank


def upper_ones():
    r = lax.broadcasted_iota(jnp.int32, (256, 256), 0)
    c = lax.broadcasted_iota(jnp.int32, (256, 256), 1)
    return jnp.where(r < c, 1.0, 0.0).astype(jnp.bfloat16)


def table_kernel(shard_ref, local_ref, tab_ref):
    upper = upper_ones()
    owner = shard_ref[...]
    value = ((owner & 1) * 64 + local_ref[...]).astype(jnp.float32)
    lane = lax.broadcasted_iota(jnp.int32, (CHIPS, 128), 1)
    acc = jnp.zeros((CHIPS, 128), jnp.float32)
    for q in range(8):
        hit, rank = matches(owner[q:q + 1] >> 1, upper)
        there = jnp.where(hit, value[q:q + 1], 0.0)
        for s in range(SLOTS):
            col = jnp.sum(jnp.where(rank == s, there, 0.0), axis=1, keepdims=True)
            acc = jnp.where(lane == q * SLOTS + s, col, acc)
    tab_ref[...] = acc.astype(jnp.int32)


def pick_kernel(shard_ref, got_ref, out_ref):
    x = lax.rem(lax.axis_index("psg"), 4)
    got = got_ref[...]
    mine = got
    for k in range(1, 4):
        mine = jnp.where(x == k, pltpu.roll(got, 128 - 32 * k, 1), mine)
    upper = upper_ones()
    owner = shard_ref[...]
    for q in range(8):
        hit, rank = matches(owner[q:q + 1] >> 1, upper)
        acc = jnp.zeros((CHIPS, 256), jnp.float32)
        for s in range(SLOTS):
            acc = jnp.where(rank == s, mine[:, q * SLOTS + s:q * SLOTS + s + 1], acc)
        out_ref[pl.ds(q, 1), :] = jnp.sum(jnp.where(hit, acc, 0.0), axis=0, keepdims=True)


def body(queries, cand_shard, cand_local, passages, lengths):
    owner = cand_shard[:, :, 0]
    slot = jnp.arange(ROWS, dtype=jnp.int32)
    wide = jnp.pad(passages, ((0, 0), (0, ROWS - passages.shape[1]), (0, 0)))
    tokens = jnp.where((slot[None, :] < lengths[:, None])[:, :, None], wide, passages[:, :1, :])
    vmem = pl.BlockSpec(memory_space=pltpu.VMEM)
    tab = pl.pallas_call(
        table_kernel, out_shape=jax.ShapeDtypeStruct((CHIPS, 128), jnp.int32),
        in_specs=[vmem, vmem], out_specs=vmem, name="table")(owner, cand_local)
    got = spread(queries, tab, tokens)
    return pl.pallas_call(
        pick_kernel, out_shape=jax.ShapeDtypeStruct(cand_local.shape, jnp.float32),
        in_specs=[vmem, vmem], out_specs=vmem, name="pick")(owner, got)


def solution(mesh):
    both = ("psg", "qry")
    in_specs = (P(both, None, None), P(both, None, None), P(both, None), P(both, None, None), P(both))
    return jax.shard_map(body, mesh=mesh, in_specs=in_specs, out_specs=P(both, None), check_vma=False)
```
